32 devices in a mesh: rows: 16 (over z, y, x), heads: 2 (over core).
Axes of the slice: x: 2, y: 2, z: 4, core: 2. Of those that a mesh axis runs over, the one named last changes fastest.
Arguments:
- tokens: bfloat16 [49152, 768], P('rows'), may hold values from -6 to 6
- cotangent: bfloat16 [49152, 768], P(('rows', 'heads')), may hold values from -6 to 6
- lengths: int32 [96], P('rows'), may hold values from 1 to 512, 29491 in all
- qkv_weight: float32 [3, 768, 768], P(None, 'rows', 'heads'), may hold values from -0.3125 to 0.3125
- qkv_first: float32 [3, 768, 768], P(None, 'rows', 'heads'), may hold values from -0.0625 to 0.0625
- qkv_second: float32 [3, 768, 768], P(None, 'rows', 'heads'), may hold values from 1.4e-06 to 5.7e-06
- out_weight: float32 [768, 768], P(('rows', 'heads')), may hold values from -0.625 to 0.625
- out_first: float32 [768, 768], P(('rows', 'heads')), may hold values from -0.0625 to 0.0625
- out_second: float32 [768, 768], P(('rows', 'heads')), may hold values from 1.4e-06 to 5.7e-06
- in_weight: float32 [768, 3072], P(('rows', 'heads')), may hold values from -0.21875 to 0.21875
- in_first: float32 [768, 3072], P(('rows', 'heads')), may hold values from -0.0625 to 0.0625
- in_second: float32 [768, 3072], P(('rows', 'heads')), may hold values from 1.4e-06 to 5.7e-06
- back_weight: float32 [3072, 768], P(('rows', 'heads')), may hold values from -0.109375 to 0.109375
- back_first: float32 [3072, 768], P(('rows', 'heads')), may hold values from -0.0625 to 0.0625
- back_second: float32 [3072, 768], P(('rows', 'heads')), may hold values from 1.4e-06 to 5.7e-06
- vectors: float32 [12, 768], replicated, may hold values from -0.8 to 1.8, as said below
- vector_first: float32 [12, 768], replicated, may hold values from -0.0625 to 0.0625
- vector_second: float32 [12, 768], replicated, may hold values from 1.4e-06 to 5.7e-06
Outputs:
- block_out: float32 [49152, 768], P(('rows', 'heads'))
- grad_in: float32 [49152, 768], P(('rows', 'heads'))
- grad_norm: float32 [1], replicated
- qkv_new: float32 [3, 768, 768], P(None, 'rows', 'heads')
- qkv_first_new: float32 [3, 768, 768], P(None, 'rows', 'heads')
- qkv_second_new: float32 [3, 768, 768], P(None, 'rows', 'heads')
- out_new: float32 [768, 768], P(('rows', 'heads'))
- out_first_new: float32 [768, 768], P(('rows', 'heads'))
- out_second_new: float32 [768, 768], P(('rows', 'heads'))
- in_new: float32 [768, 3072], P(('rows', 'heads'))
- in_first_new: float32 [768, 3072], P(('rows', 'heads'))
- in_second_new: float32 [768, 3072], P(('rows', 'heads'))
- back_new: float32 [3072, 768], P(('rows', 'heads'))
- back_first_new: float32 [3072, 768], P(('rows', 'heads'))
- back_second_new: float32 [3072, 768], P(('rows', 'heads'))
- vectors_new: float32 [12, 768], replicated
- vector_first_new: float32 [12, 768], replicated
- vector_second_new: float32 [12, 768], replicated
The draws below stay inside these ranges and needn't reach their ends.
Inputs may be any that keep to these rules, and one draw needn't show every extreme that they name: Each sequence's keys at positions lengths[i] and beyond are masked; the longest sequence has exactly 512. `vectors`: rows 3 and 6 are the norms' gains, the other rows biases.
All inputs are finite; a program needn't handle non-finite values. No bound on the sum of `lengths` on one device may be relied on, other than what follows from the above.
Results may differ from the reference program's by a relative error of at most 0.015.
The reference program's roundings to bfloat16 on the way count: a program that leaves them out, or rounds other values in their place, can miss the bound.
Values may be sent and summed in bfloat16 or wider, within the bound.
No kernel may reach another device: no remote copies, remote signals or barrier semaphores. Data moves between devices by JAX's collectives and lax.ppermute only.
A program may use at most 192 MiB of HBM per device.

```python
import math
import jax
import jax.numpy as jnp
import numpy as np
from jax import lax

D = 768
FF = 3072
ATT_HEADS = 12
HEAD_DIM = 64
SEQ_LEN = 512
SEQ_DEV = 6
SEQS = 96
TOKENS = 49152
VEC_ROWS = 12
N_ROWS = 16


def draw_vectors(key, part):
    shape = (VEC_ROWS, D)
    base = jnp.clip(0.2 * jax.random.normal(key, shape, jnp.float32), -0.8, 0.8)
    places = lax.broadcasted_iota(jnp.int32, shape, 0)
    lifted = jnp.where((places == 3) | (places == 6), 1.0, 0.0).astype(jnp.float32)
    return base + lifted


def with_spikes(values, stream_key, source, target, parts, factor):
    owner, partner = [(jnp.arange(values.shape[dim]) // (values.shape[dim] // parts)).reshape([-1 if axis == dim else 1 for axis in range(values.ndim)]) for dim in (source, target)]
    chosen = jax.random.permutation(stream_key, parts)[partner]
    strong = (owner == chosen) | (owner == (partner + parts // 2) % parts)
    return jnp.where(strong, factor * values, values)


def block_levels(stream_key, shape, split, least, high):
    def one(axis_at, parts):
        draws = jax.random.uniform(jax.random.fold_in(jax.random.fold_in(stream_key, 6), axis_at), (parts,), jnp.float32, least / len(split), high / len(split))
        return jnp.repeat(jnp.exp(draws), shape[axis_at] // parts).reshape((-1,) + (1,) * (len(shape) - axis_at - 1))

    factor_of = one(*split[0])
    for cut in split[1:]:
        factor_of = factor_of * one(*cut)
    return factor_of


def length_profile(amount, total, reach, lean):
    weights = [(1 << 20) // math.isqrt(rank ** lean) + 1 for rank in range(2, amount + 1)]
    rest, counts = total - reach - (amount - 1), [1] * (amount - 1)
    while rest > 0:
        free = [i for i in range(amount - 1) if counts[i] < reach]
        whole, remaining = sum([weights[i] for i in free]), rest
        for i in free:
            addition = min(reach - counts[i], max(1, remaining * weights[i] // whole), rest)
            counts[i] = counts[i] + addition
            rest = rest - addition
    return np.array([reach] + counts)


def uneven_parts(stream_key, count, total, bound, skew):
    if count == 2:
        one = jax.random.randint(stream_key, (), max(1, total - bound), min(bound, total - 1) + 1)
        return jnp.stack([one, total - one])
    sizes = jnp.asarray(length_profile(count, total, bound, skew), jnp.int32)
    couples = (count - 1) // 2
    giver, receiver = sizes[1:1 + 2 * couples:2], sizes[2:2 + 2 * couples:2]
    margin = jnp.minimum(giver - 1, bound - receiver)
    shifted = jax.random.randint(jax.random.fold_in(stream_key, 1), (couples,), 0, 1 << 20) % (margin + 1)
    sizes = sizes.at[1:1 + 2 * couples:2].set(giver - shifted).at[2:2 + 2 * couples:2].set(receiver + shifted)
    return sizes[jax.random.permutation(jax.random.fold_in(stream_key, 2), count)]


def centred(key, extent, scale, most, split=(), kind=jnp.bfloat16):
    factor_of = block_levels(key, extent, split, -0.22, 0.18) if split else 1.0
    values = jax.random.normal(key, extent, jnp.float32) * scale * factor_of
    return jnp.minimum(jnp.maximum(values, -most), most).astype(kind)


def gaussian_with(key, extent, width, reach, shards, heavy, kind=jnp.bfloat16):
    values = width * jax.random.normal(key, extent, jnp.float32)
    if shards:
        values = values * block_levels(key, extent, shards, -0.22, 0.18)
    return jnp.clip(with_spikes(values, jax.random.fold_in(key, 3), *heavy), -reach, reach).astype(kind)


def setup_inputs(seed: int = 0) -> dict:
    key_of = jax.random.split(jax.random.key(seed), 19)
    return {
        "tokens": gaussian_with(key_of[0], (TOKENS, D), 1.0, 6.0, ((0, 16),), (0, 1, 16, 2.0)),
        "cotangent": centred(key_of[1], (TOKENS, D), 1.0, 6.0, ((0, 32),)),
        "lengths": uneven_parts(key_of[2], SEQS, SEQS * SEQ_LEN * 3 // 5, SEQ_LEN, 2).astype(jnp.int32),
        "qkv_weight": centred(key_of[3], (3, D, D), (D // 2) ** -0.5, 0.3125, ((1, 16), (2, 2)), jnp.float32),
        "qkv_first": centred(key_of[4], (3, D, D), 0.004, 0.0625, ((1, 16), (2, 2)), jnp.float32),
        "qkv_second": jnp.clip(jnp.exp(math.log(5.700000201613875e-06) - 1.403994 * jax.random.uniform(key_of[5], (3, D, D), jnp.float32) ** block_levels(key_of[5], (3, D, D), ((1, 16), (2, 2)), -0.2, 0.2)), 1.3999999737279722e-06, 5.700000201613875e-06),
        "out_weight": centred(key_of[6], (D, D), (D // 8) ** -0.5, 0.625, ((0, 32),), jnp.float32),
        "out_first": centred(key_of[7], (D, D), 0.004, 0.0625, ((0, 32),), jnp.float32),
        "out_second": jnp.clip(jnp.exp(math.log(5.700000201613875e-06) - 1.403994 * jax.random.uniform(key_of[8], (D, D), jnp.float32) ** block_levels(key_of[8], (D, D), ((0, 32),), -0.2, 0.2)), 1.3999999737279722e-06, 5.700000201613875e-06),
        "in_weight": centred(key_of[9], (D, FF), D ** -0.5, 0.21875, ((0, 32),), jnp.float32),
        "in_first": centred(key_of[10], (D, FF), 0.004, 0.0625, ((0, 32),), jnp.float32),
        "in_second": jnp.clip(jnp.exp(math.log(5.700000201613875e-06) - 1.403994 * jax.random.uniform(key_of[11], (D, FF), jnp.float32) ** block_levels(key_of[11], (D, FF), ((0, 32),), -0.2, 0.2)), 1.3999999737279722e-06, 5.700000201613875e-06),
        "back_weight": centred(key_of[12], (FF, D), FF ** -0.5, 0.109375, ((0, 32),), jnp.float32),
        "back_first": centred(key_of[13], (FF, D), 0.004, 0.0625, ((0, 32),), jnp.float32),
        "back_second": jnp.clip(jnp.exp(math.log(5.700000201613875e-06) - 1.403994 * jax.random.uniform(key_of[14], (FF, D), jnp.float32) ** block_levels(key_of[14], (FF, D), ((0, 32),), -0.2, 0.2)), 1.3999999737279722e-06, 5.700000201613875e-06),
        "vectors": draw_vectors(jax.random.fold_in(key_of[18], 71), 0),
        "vector_first": centred(key_of[16], (VEC_ROWS, D), 0.004, 0.0625, (), jnp.float32),
        "vector_second": jnp.clip(jnp.exp(jax.random.uniform(key_of[17], (VEC_ROWS, D), jnp.float32, math.log(1.3999999737279722e-06), math.log(5.700000201613875e-06))), 1.3999999737279722e-06, 5.700000201613875e-06),
    }


@jax.custom_vjp
def low(v):
    return lax.optimization_barrier(v.astype(jnp.bfloat16)).astype(jnp.float32)

@jax.custom_vjp
def low_back(v):
    return v

def low_keep(v):
    return (low(v), None)

def low_pass(kept, grad):
    return (grad,)

def back_keep(v):
    return (v, None)

def back_low(kept, grad):
    return (low(grad),)
low.defvjp(low_keep, low_pass)
low_back.defvjp(back_keep, back_low)
eps_norm = 1e-12
clip_limit = 100.0
learn_rate = 0.08
vector_rate = 0.3
beta_one = 0.9
beta_two = 0.999
adam_eps = 1e-06
decay_rate = 0.01
step_count = 10

def matmul(left, right):
    return jnp.dot(left, right, precision=lax.Precision.HIGHEST, preferred_element_type=jnp.float32)

def layer_norm(values, gain, shift):
    center = values - lax.optimization_barrier(jnp.mean(values, axis=-1, keepdims=True))
    spread = lax.optimization_barrier(jnp.mean(center * center, axis=-1, keepdims=True))
    return center * lax.rsqrt(spread + eps_norm) * gain + shift

def attention(queries, key_rows, value_rows, spans):
    scores = jnp.einsum('gqhe,gkhe->ghqk', queries, key_rows, precision=lax.Precision.HIGHEST)
    scores = low_back(scores * HEAD_DIM ** (-0.5))
    places = lax.broadcasted_iota(jnp.int32, (1, 1, 1, SEQ_LEN), 3)
    scores = jnp.where(places < spans[:, None, None, None], scores, -1000000000.0)
    highest = lax.optimization_barrier(jnp.max(scores, axis=-1, keepdims=True))
    weights = jnp.exp(scores - highest)
    probs = weights / lax.optimization_barrier(jnp.sum(weights, axis=-1, keepdims=True))
    return jnp.einsum('ghqk,gkhe->gqhe', low(probs), value_rows, precision=lax.Precision.HIGHEST)

def group_forward(spans, inputs, qkv_weight, out_weight, in_weight, back_weight, vectors):
    count = inputs.shape[0]
    groups = count // SEQ_LEN
    w_query = low(qkv_weight[0])
    w_key = low(qkv_weight[1])
    w_value = low(qkv_weight[2])
    w_output = low(out_weight)
    w_inner = low(in_weight)
    w_outer = low(back_weight)
    query = low(low_back(matmul(inputs, w_query) + vectors[0]))
    key_proj = low(low_back(matmul(inputs, w_key)))
    value = low(low_back(matmul(inputs, w_value) + vectors[1]))
    shape = (groups, SEQ_LEN, ATT_HEADS, HEAD_DIM)
    context = jax.checkpoint(attention)(query.reshape(shape), key_proj.reshape(shape), value.reshape(shape), spans)
    context = low(low_back(context.reshape(count, D)))
    attn_out = low_back(matmul(context, w_output) + vectors[2])
    hidden = layer_norm(inputs + attn_out, vectors[3], vectors[4])
    inner = low_back(matmul(low(hidden), w_inner) + vectors[8:].reshape(FF))
    activ = low(jax.nn.gelu(inner, approximate=False))
    ffn_out = low_back(matmul(activ, w_outer) + vectors[5])
    return layer_norm(hidden + ffn_out, vectors[6], vectors[7])

def adam_update(weight, first, second, grad, decay, rate):
    first_new = beta_one * first + (1.0 - beta_one) * grad
    second_new = beta_two * second + (1.0 - beta_two) * grad * grad
    fix_one = 1.0 - beta_one ** step_count
    fix_two = 1.0 - beta_two ** step_count
    move = first_new / fix_one / (jnp.sqrt(second_new / fix_two) + adam_eps)
    return (weight - rate * (move + decay * weight), first_new, second_new)

def reference(tokens, cotangent, lengths, qkv_weight, qkv_first, qkv_second, out_weight, out_first, out_second, in_weight, in_first, in_second, back_weight, back_first, back_second, vectors, vector_first, vector_second):
    group_seqs = 8
    groups = SEQ_DEV * N_ROWS // group_seqs
    inputs = tokens.astype(jnp.float32).reshape(groups, group_seqs * SEQ_LEN, D)
    upstream = cotangent.astype(jnp.float32).reshape(groups, group_seqs * SEQ_LEN, D)
    spans = lengths.astype(jnp.int32).reshape(groups, group_seqs)
    params = (qkv_weight, out_weight, in_weight, back_weight, vectors)

    def accumulate(totals, item):
        piece, pulled, span = item

        def forward(inputs_group, *weights):
            return group_forward(span, inputs_group, *weights)
        result, pullback = jax.vjp(forward, piece, *params)
        grads = pullback(pulled)
        return (tuple((total + extra for total, extra in zip(totals, grads[1:]))), (result, grads[0]))
    start = tuple((jnp.zeros_like(weight) for weight in params))
    totals, (outputs, input_grads) = lax.scan(accumulate, start, (inputs, upstream, spans))
    squares = jnp.sum(totals[0] * totals[0]) + jnp.sum(totals[1] * totals[1]) + jnp.sum(totals[2] * totals[2]) + jnp.sum(totals[3] * totals[3]) + jnp.sum(totals[4] * totals[4])
    grad_norm = jnp.sqrt(squares)
    factor = clip_limit / jnp.maximum(grad_norm, clip_limit)
    qkv_new = adam_update(qkv_weight, qkv_first, qkv_second, factor * totals[0], decay_rate, learn_rate)
    out_new = adam_update(out_weight, out_first, out_second, factor * totals[1], decay_rate, learn_rate)
    in_new = adam_update(in_weight, in_first, in_second, factor * totals[2], decay_rate, learn_rate)
    back_new = adam_update(back_weight, back_first, back_second, factor * totals[3], decay_rate, learn_rate)
    vec_new = adam_update(vectors, vector_first, vector_second, factor * totals[4], 0.0, vector_rate)
    return (outputs.reshape(TOKENS, D), input_grads.reshape(TOKENS, D), grad_norm.reshape(1), qkv_new[0], qkv_new[1], qkv_new[2], out_new[0], out_new[1], out_new[2], in_new[0], in_new[1], in_new[2], back_new[0], back_new[1], back_new[2], vec_new[0], vec_new[1], vec_new[2])
```

```python
import jax
import jax.numpy as jnp
from jax import lax
from jax.experimental import pallas as pl
from jax.experimental.pallas import tpu as pltpu
from jax.sharding import PartitionSpec as P

HEAD_DIM = 64
BF = jnp.bfloat16
F32 = jnp.float32
eps_norm = 1e-12


def nn(a, b):
    return jnp.dot(a, b, preferred_element_type=F32)


def nt(a, b):
    return lax.dot_general(a, b, (((1,), (1,)), ((), ())), preferred_element_type=F32)


def tn(a, b):
    return lax.dot_general(a, b, (((0,), (0,)), ((), ())), preferred_element_type=F32)


X, Y = 1, 2
Z = (0, 4, 8, 12)
PIECES = lambda first, second: tuple(
    tuple(z ^ b for z in Z) for b in (0, first, second, first ^ second))


def copy_blocks(pieces, orders, row, sem, place):
    for stream, refs in enumerate(pieces):
        masks = PIECES(*orders[stream])
        for ref, group in zip(refs, masks):
            for i, mask in enumerate(group):
                for src, dst in place(ref, stream, i, row ^ mask):
                    pltpu.make_async_copy(src, dst, sem).start()


QKV_SPLIT = (80, 64)
STREAMS = ((X, Y), (Y, X))


def qkv_place(target, cols, block):
    cut = QKV_SPLIT[0] - block

    def place(ref, stream, i, chip):
        size = QKV_SPLIT[stream]
        at = pl.multiple_of(chip * block, 16)
        piece = lambda a, b: ref.at[pl.ds(i * size + a, b - a)]
        into = lambda j, a, b: target.at[pl.ds(at + a, b - a), pl.ds(j * cols, cols)]
        if stream == 0:
            return ((piece(0, block), into(0, 0, block)), (piece(block, size), into(1, 0, cut)))
        rest = block - cut
        return ((piece(0, rest), into(1, cut, block)), (piece(rest, size), into(2, 0, block)))

    return place


def lane_mask(width, which):
    lanes = lax.broadcasted_iota(jnp.int32, (1, width), 1)
    return jnp.where(lanes // HEAD_DIM == which, 1.0, 0.0).astype(BF)


def key_rows_valid(keys, queries, length):
    return lax.broadcasted_iota(jnp.int32, (keys, queries), 0) < length


def attn_fwd_kernel(fast, info, lens, x_ref, vec_ref, *refs):
    half, seq = pl.program_id(0), pl.program_id(1)
    if fast:
        pieces, (ctx_ref, q_ref, k_ref, v_ref, lse_ref, w_ref, all_ref, sem) = refs[:16], refs[16:]
        block = all_ref.shape[1] // 16

        @pl.when((half == 0) & (seq == 0))
        def _():
            for i in range(2):
                own = pieces[8 * i:8 * i + 8]
                copy_blocks((own[:4], own[4:]), STREAMS, info[1], sem.at[i],
                            qkv_place(all_ref.at[i], ctx_ref.shape[1], block))

        for i in range(2):
            @pl.when((half == i) & (seq == 0))
            def _():
                pltpu.make_async_copy(all_ref.at[i], all_ref.at[i], sem.at[i]).wait()

        weights = all_ref[half]

        @pl.when(seq == 0)
        def _():
            w_ref[...] = weights
    else:
        w_ref, ctx_ref, q_ref, k_ref, v_ref, lse_ref = refs
        weights = w_ref[...]
    core = info[0]
    length = lens[core * pl.num_programs(1) + seq]
    cols = ctx_ref.shape[1]
    keys = x_ref.shape[0]
    start = pl.multiple_of((core ^ half) * cols, 128)
    proj = nn(x_ref[...], weights)
    q = (proj[:, :cols] + vec_ref[0:1, pl.ds(start, cols)]).astype(BF) * BF(HEAD_DIM ** -0.5)
    k = proj[:, cols:2 * cols].astype(BF)
    v = (proj[:, 2 * cols:] + vec_ref[1:2, pl.ds(start, cols)]).astype(BF)
    q_ref[...] = q
    k_ref[...] = k
    v_ref[...] = v
    valid = key_rows_valid(keys, keys, length)
    for pair in range(cols // 128):
        span = slice(128 * pair, 128 * pair + 128)
        kp, qp = k[:, span], q[:, span]
        vt = v[:, span].T
        parts = []
        for sub in range(2):
            s = nt(kp, qp * lane_mask(128, sub))
            s = jnp.where(valid, s, -1000000000.0)
            top = jnp.max(s, axis=0, keepdims=True)
            e = jnp.exp(s - top)
            total = jnp.sum(e, axis=0, keepdims=True)
            p = (e * (1.0 / total)).astype(BF)
            lse_ref[pl.ds(2 * pair + sub, 1), :] = top + jnp.log(total)
            parts.append(nn(vt[HEAD_DIM * sub:HEAD_DIM * sub + HEAD_DIM, :], p))
        ctx_ref[:, span] = jnp.concatenate(parts, axis=0).T.astype(BF)


def attn_fwd(info, lengths, tokens, wqkv, vectors, seqs, seq_len, cols):
    model = tokens.shape[1]
    tok = seqs * seq_len
    fast = len(wqkv) > 1
    weight = pl.BlockSpec((None, model, 3 * cols), lambda h, s, info, lens: (h, 0, 0))
    anywhere = pl.BlockSpec(memory_space=pl.ANY)
    grid_spec = pltpu.PrefetchScalarGridSpec(
        num_scalar_prefetch=2,
        grid=(2, seqs),
        in_specs=[
            pl.BlockSpec((seq_len, model), lambda h, s, info, lens: (info[0] * seqs + s, 0)),
            pl.BlockSpec(vectors.shape, lambda h, s, info, lens: (0, 0)),
        ] + ([anywhere] * len(wqkv) if fast else [weight]),
        out_specs=[
            pl.BlockSpec((seq_len, cols), lambda h, s, info, lens: (s, info[0] ^ h)),
            pl.BlockSpec((None, seq_len, cols), lambda h, s, info, lens: (h, s, 0)),
            pl.BlockSpec((None, seq_len, cols), lambda h, s, info, lens: (h, s, 0)),
            pl.BlockSpec((None, seq_len, cols), lambda h, s, info, lens: (h, s, 0)),
            pl.BlockSpec((None, None, 8, seq_len), lambda h, s, info, lens: (h, s, 0, 0)),
        ] + ([weight] if fast else []),
        scratch_shapes=[pltpu.VMEM((2, model, 3 * cols), BF), pltpu.SemaphoreType.DMA((2,))] if fast else [],
    )
    half_shape = jax.ShapeDtypeStruct((2, tok, cols), BF)
    return pl.pallas_call(
        lambda *refs: attn_fwd_kernel(fast, *refs),
        grid_spec=grid_spec,
        out_shape=[
            jax.ShapeDtypeStruct((tok, 2 * cols), BF),
            half_shape, half_shape, half_shape,
            jax.ShapeDtypeStruct((2, seqs, 8, seq_len), F32),
        ] + ([jax.ShapeDtypeStruct((2, model, 3 * cols), BF)] if fast else []),
        compiler_params=pltpu.CompilerParams(vmem_limit_bytes=48 << 20),
        cost_estimate=pl.CostEstimate(flops=25 * 10**9, transcendentals=tok * seq_len * 12,
                                      bytes_accessed=2 * 10 * tok * cols),
        name="attention_forward",
    )(info, lengths, tokens, vectors, *wqkv)


def attn_bwd_kernel(half, store, info, lens, x_ref, q_ref, k_ref, v_ref, dctx_ref, lse_ref,
                    dqkv_ref, bias_ref, *rest):
    seq = pl.program_id(0)
    core = info[0]
    length = lens[core * pl.num_programs(0) + seq]
    keys, cols = q_ref.shape
    valid = key_rows_valid(keys, keys, length)
    q, k, v, dc = q_ref[...], k_ref[...], v_ref[...], dctx_ref[...]
    for pair in range(cols // 128):
        span = slice(128 * pair, 128 * pair + 128)
        kp, qp, vp, dp_ = k[:, span], q[:, span], v[:, span], dc[:, span]
        kt, qt, dt = kp.T, qp.T, dp_.T
        dq, dk, dv = [], [], []
        for sub in range(2):
            rows = slice(HEAD_DIM * sub, HEAD_DIM * sub + HEAD_DIM)
            mask = lane_mask(128, sub)
            s = nt(kp, qp * mask)
            p = jnp.where(valid, jnp.exp(s - lse_ref[pl.ds(2 * pair + sub, 1), :]), 0.0)
            dv.append(nt(dt[rows, :], p.astype(BF)))
            dprob = nt(vp, dp_ * mask)
            delta = jnp.sum(p * dprob, axis=0, keepdims=True)
            ds = (p * (dprob - delta)).astype(BF)
            dk.append(nt(qt[rows, :], ds))
            dq.append(nn(kt[rows, :], ds) * HEAD_DIM ** -0.5)
        for j, val in enumerate((dq, dk, dv)):
            low = jnp.concatenate(val, axis=0).T.astype(BF)
            dqkv_ref[:, j * cols + 128 * pair:j * cols + 128 * pair + 128] = low
    low = dqkv_ref[...]

    @pl.when(seq == 0)
    def _():
        bias_ref[...] = jnp.zeros_like(bias_ref)

    bias_ref[0:1, :] += jnp.sum(low[:, :cols].astype(F32), axis=0, keepdims=True)
    bias_ref[1:2, :] += jnp.sum(low[:, 2 * cols:].astype(F32), axis=0, keepdims=True)
    if store:
        one_ref, two_ref, acc = rest
        grad = tn(x_ref[...], low)

        @pl.when(seq == 0)
        def _():
            acc[...] = grad

        @pl.when(seq > 0)
        def _():
            acc[...] += grad

        @pl.when(seq == pl.num_programs(0) - 1)
        def _():
            store(info, acc, one_ref, two_ref)


def attn_bwd(half, info, lengths, tokens, q, k, v, dctx, lse, seqs, seq_len, store=None, shapes=()):
    model = tokens.shape[1]
    cols = q.shape[2]
    tok = seqs * seq_len
    head = pl.BlockSpec((None, seq_len, cols), lambda s, info, lens: (half, s, 0))
    whole = lambda shape: pl.BlockSpec(shape, lambda s, info, lens: (0,) * len(shape))
    out_specs = [
        pl.BlockSpec((seq_len, 3 * cols), lambda s, info, lens: (s, 0)),
        whole((8, cols)),
    ]
    out_shape = [jax.ShapeDtypeStruct((tok, 3 * cols), BF), jax.ShapeDtypeStruct((8, cols), F32)]
    scratch = []
    if store:
        out_specs += [whole(s.shape) for s in shapes]
        out_shape += list(shapes)
        scratch = [pltpu.VMEM((model, 3 * cols), F32)]
    grid_spec = pltpu.PrefetchScalarGridSpec(
        num_scalar_prefetch=2,
        grid=(seqs,),
        in_specs=[
            pl.BlockSpec((seq_len, model), lambda s, info, lens: (info[0] * seqs + s, 0)),
            head, head, head,
            pl.BlockSpec((seq_len, cols), lambda s, info, lens: (s, info[0] ^ half)),
            pl.BlockSpec((None, None, 8, seq_len), lambda s, info, lens: (half, s, 0, 0)),
        ],
        out_specs=out_specs,
        scratch_shapes=scratch,
    )
    return pl.pallas_call(
        lambda *refs: attn_bwd_kernel(half, store, *refs),
        grid_spec=grid_spec,
        out_shape=out_shape,
        compiler_params=pltpu.CompilerParams(vmem_limit_bytes=48 << 20),
        cost_estimate=pl.CostEstimate(flops=25 * 10**9, transcendentals=tok * seq_len * 6,
                                      bytes_accessed=2 * 10 * tok * cols),
        name="attention_backward",
    )(info, lengths, tokens, q, k, v, dctx, lse)


TAIL_SCALE = 0.3 / 2 ** 0.5
TAIL_POLY = (0.16918733802338345, 0.17072502265423276, 0.14827808314028249, 0.215137650024653,
             -0.09509659092542666, 0.5483061894891728, -0.5127483189659462, 0.48577399370156327,
             -0.12956338680438764)


def gelu_pair(u):
    t = 1.0 / (1.0 + TAIL_SCALE * jnp.abs(u))
    bell = jnp.exp(u * u * -0.5)
    poly = jnp.full_like(u, 0.5 * TAIL_POLY[-1])
    for c in TAIL_POLY[-2::-1]:
        poly = poly * t + 0.5 * c
    tail = poly * t * bell
    cdf = jnp.where(u < 0.0, tail, 1.0 - tail)
    return u * cdf, cdf + u * (bell * (2.0 * 3.141592653589793) ** -0.5)


def norm_stats(z):
    center = z - jnp.mean(z, axis=-1, keepdims=True)
    r = lax.rsqrt(jnp.mean(center * center, axis=-1, keepdims=True) + eps_norm)
    return center * r, r


def norm_back(dy, xhat, r, gain):
    e = dy * gain
    return r * (e - jnp.mean(e, axis=-1, keepdims=True)
                - xhat * jnp.mean(e * xhat, axis=-1, keepdims=True))


def colsum(a):
    return jnp.sum(a, axis=0, keepdims=True)


def ffn_place(targets, core):
    wo, w1, w2 = targets
    model, inner = w1.shape
    block = model // 16
    wide, narrow = inner // 2, model // 2

    def place(ref, stream, i, chip):
        rows = pl.ds(i * block, block)
        if stream == 0:
            at = pl.ds(pl.multiple_of(chip * block, 16), block)
            left = pl.ds(pl.multiple_of(core * wide, 128), wide)
            right = pl.ds(pl.multiple_of(core * narrow, 128), narrow)
            return ((ref.at[rows, pl.ds(0, wide)], w1.at[at, left]),
                    (ref.at[rows, pl.ds(wide, narrow)], wo.at[at, right]))
        at = (chip * 2 + core) * (2 * block)
        return tuple((ref.at[rows, pl.ds(j * model, model)],
                      w2.at[pl.ds(pl.multiple_of(at + j * block, 16), block)]) for j in range(2))

    return place


def ffn_kernel(chunk, fast, info, x_ref, ctx_ref, cot_ref, vec_ref, b1_ref, *refs):
    step = pl.program_id(0)
    if fast:
        pieces, refs = refs[:16], refs[16:]
        both_ref, w2_ref, sem = refs[-3:]
        refs = refs[:-3]
        wide = both_ref.shape[1] - both_ref.shape[0]
        w1_ref, wo_ref = both_ref.at[:, :wide], both_ref.at[:, wide:]

        @pl.when(step == 0)
        def _():
            for i in range(2):
                half = pieces[8 * i:8 * i + 8]
                place = ffn_place((wo_ref, w1_ref, w2_ref), info[0] ^ i)
                copy_blocks((half[:4],), STREAMS[:1], info[1], sem.at[0], place)
            for i in range(2):
                half = pieces[8 * i:8 * i + 8]
                place = ffn_place((wo_ref, w1_ref, w2_ref), info[0] ^ i)
                copy_blocks(((), half[4:]), STREAMS, info[1], sem.at[1], place)
            pltpu.make_async_copy(both_ref, both_ref, sem.at[0]).wait()
            pltpu.make_async_copy(w2_ref, w2_ref, sem.at[1]).wait()
    else:
        wo_ref, w1_ref, w2_ref, *refs = refs
    (out_ref, dz1_ref, dctx_ref, h_ref, g_ref, df_ref, du_ref, da_ref, vg_ref, b1g_ref,
     slope_ref) = refs
    inner = w1_ref.shape[1]

    @pl.when(step == 0)
    def _():
        vg_ref[...] = jnp.zeros_like(vg_ref)
        b1g_ref[...] = jnp.zeros_like(b1g_ref)

    z1 = x_ref[...].astype(F32) + nn(ctx_ref[...], wo_ref[...]) + vec_ref[2:3, :]
    xhat1, r1 = norm_stats(z1)
    h = xhat1 * vec_ref[3:4, :] + vec_ref[4:5, :]
    h_low = h.astype(BF)
    h_ref[...] = h_low
    z2 = h + vec_ref[5:6, :]
    for j in range(inner // chunk):
        span = slice(j * chunk, j * chunk + chunk)
        u = nn(h_low, w1_ref[:, span]) + b1_ref[:, span]
        g, slope = gelu_pair(u)
        g = g.astype(BF)
        g_ref[:, span] = g
        slope_ref[:, span] = slope
        z2 = z2 + nn(g, w2_ref[span, :])
    xhat2, r2 = norm_stats(z2)
    out_ref[...] = xhat2 * vec_ref[6:7, :] + vec_ref[7:8, :]
    dy = cot_ref[...].astype(F32)
    vg_ref[4:5, :] += colsum(dy * xhat2)
    vg_ref[5:6, :] += colsum(dy)
    dz2 = norm_back(dy, xhat2, r2, vec_ref[6:7, :])
    df = dz2.astype(BF)
    df_ref[...] = df
    vg_ref[3:4, :] += colsum(df.astype(F32))
    dh = dz2
    for j in range(inner // chunk):
        span = slice(j * chunk, j * chunk + chunk)
        du = (nt(df, w2_ref[span, :]) * slope_ref[:, span]).astype(BF)
        du_ref[:, span] = du
        b1g_ref[:, span] += colsum(du.astype(F32))
        dh = dh + nt(du, w1_ref[:, span])
    vg_ref[1:2, :] += colsum(dh * xhat1)
    vg_ref[2:3, :] += colsum(dh)
    dz1 = norm_back(dh, xhat1, r1, vec_ref[3:4, :])
    dz1_ref[...] = dz1
    da = dz1.astype(BF)
    da_ref[...] = da
    vg_ref[0:1, :] += colsum(da.astype(F32))
    dctx_ref[...] = nt(da, wo_ref[...]).astype(BF)


def ffn(info, tokens, ctx, cotangent, weights, vectors, tile=256, chunk=768):
    tok, model = cotangent.shape
    inner = (vectors.shape[0] - 8) * model
    steps = tok // tile
    fast = len(weights) > 3
    row = pl.BlockSpec((tile, model), lambda s, info: (s, 0))
    wide = pl.BlockSpec((tile, inner), lambda s, info: (s, 0))
    whole = lambda shape: pl.BlockSpec(shape, lambda s, info: (0, 0), pipeline_mode=pl.Buffered(1))
    acc = lambda shape: pl.BlockSpec(shape, lambda s, info: (0, 0))
    grid_spec = pltpu.PrefetchScalarGridSpec(
        num_scalar_prefetch=1,
        grid=(steps,),
        in_specs=[
            pl.BlockSpec((tile, model), lambda s, info: (info[0] * steps + s, 0)),
            row, row, whole((8, model)), whole((1, inner)),
        ] + [pl.BlockSpec(memory_space=pl.ANY) if fast else whole(w.shape) for w in weights],
        out_specs=[row, row, row, row, wide, row, wide, row, acc((8, model)), acc((1, inner))],
        scratch_shapes=[pltpu.VMEM((tile, inner), F32)] + ([
            pltpu.VMEM((model, inner + model), BF), pltpu.VMEM((inner, model), BF),
            pltpu.SemaphoreType.DMA((2,))] if fast else []),
    )
    f = lambda d, dt: jax.ShapeDtypeStruct((tok, d), dt)
    return pl.pallas_call(
        lambda *refs: ffn_kernel(chunk, fast, *refs),
        grid_spec=grid_spec,
        out_shape=[f(model, F32), f(model, F32), f(model, BF), f(model, BF), f(inner, BF),
                   f(model, BF), f(inner, BF), f(model, BF),
                   jax.ShapeDtypeStruct((8, model), F32), jax.ShapeDtypeStruct((1, inner), F32)],
        compiler_params=pltpu.CompilerParams(vmem_limit_bytes=58 << 20),
        cost_estimate=pl.CostEstimate(flops=60 * 10**9, transcendentals=2 * tok * inner,
                                      bytes_accessed=tok * (4 * inner + 24 * model)),
        name="feed_forward",
    )(info, tokens, ctx, cotangent, vectors[:8], vectors[8:].reshape(1, -1), *weights)


def slot(first, second, chip, row):
    j = chip ^ row
    bit = lambda b: (j >> (b - 1)) & 1
    return bit(first) * 8 + bit(second) * 4 + (j >> 2)


def store_pair(info, order, chip, first_core, second_core, own_ref, other_ref):
    at = slot(*order, chip, info[1])
    even = info[0] == 0
    own_ref[at] = jnp.where(even, first_core, second_core).astype(BF)
    other_ref[at] = jnp.where(even, second_core, first_core).astype(BF)


def back_grad_kernel(order, info, g_ref, df_ref, own_ref, other_ref):
    step = pl.program_id(0)
    grad = tn(g_ref[...], df_ref[...])
    size = own_ref.shape[1]
    chips = grad.shape[0] // (2 * size)
    for i in range(chips):
        a, b = 2 * i * size, (2 * i + 1) * size
        store_pair(info, order, step * chips + i, grad[a:b], grad[b:b + size], own_ref, other_ref)


def back_grad(info, g, df, order, steps=4):
    tok, inner = g.shape
    model = df.shape[1]
    shape = jax.ShapeDtypeStruct((16, inner // 32, model), BF)
    full = pl.BlockSpec(shape.shape, lambda s, info: (0, 0, 0))
    return pl.pallas_call(
        lambda *refs: back_grad_kernel(order, *refs),
        grid_spec=pltpu.PrefetchScalarGridSpec(
            num_scalar_prefetch=1,
            grid=(steps,),
            in_specs=[pl.BlockSpec((tok, inner // steps), lambda s, info: (0, s)),
                      pl.BlockSpec((tok, model), lambda s, info: (0, 0))],
            out_specs=[full, full],
        ),
        out_shape=[shape, shape],
        compiler_params=pltpu.CompilerParams(vmem_limit_bytes=48 << 20),
        cost_estimate=pl.CostEstimate(flops=2 * tok * inner * model, transcendentals=0,
                                      bytes_accessed=2 * (tok * (inner + model) + inner * model)),
        name="back_grad",
    )(info, g, df)


def in_grad_kernel(order, info, h_ref, du_ref, ctx_ref, da_ref, own_ref, other_ref):
    step = pl.program_id(0)
    last = pl.num_programs(0) - 1

    def put(grad):
        size = own_ref.shape[1]
        for chip in range(16):
            a, b = 2 * chip * size, (2 * chip + 1) * size
            store_pair(info, order, chip, grad[a:b], grad[b:b + size], own_ref, other_ref)

    @pl.when(step < last)
    def _():
        put(tn(h_ref[...], du_ref[...]))

    @pl.when(step == last)
    def _():
        put(tn(ctx_ref[...], da_ref[...]))


def in_grad(info, h, du, ctx, da, order):
    tok, model = h.shape
    inner = du.shape[1]
    steps = inner // model
    shape = jax.ShapeDtypeStruct((16, model // 32, inner + model), BF)
    full = pl.BlockSpec((tok, model), lambda s, info: (0, 0))
    out = pl.BlockSpec((16, model // 32, model), lambda s, info: (0, 0, s))
    return pl.pallas_call(
        lambda *refs: in_grad_kernel(order, *refs),
        grid_spec=pltpu.PrefetchScalarGridSpec(
            num_scalar_prefetch=1,
            grid=(steps + 1,),
            in_specs=[full, pl.BlockSpec((tok, model), lambda s, info: (0, jnp.minimum(s, steps - 1))),
                      full, full],
            out_specs=[out, out],
        ),
        out_shape=[shape, shape],
        compiler_params=pltpu.CompilerParams(vmem_limit_bytes=48 << 20),
        cost_estimate=pl.CostEstimate(flops=2 * tok * model * (inner + model), transcendentals=0,
                                      bytes_accessed=2 * (tok * (inner + 3 * model) + model * (inner + model))),
        name="in_grad",
    )(info, h, du, ctx, da)


def store_qkv(info, acc, one_ref, two_ref):
    cols = one_ref.shape[2]
    block = acc.shape[0] // 16
    cut = QKV_SPLIT[0] - block
    rest = block - cut
    for chip in range(16):
        one, two = (slot(*order, chip, info[1]) for order in STREAMS)
        q, k, v = (acc[block * chip:block * chip + block, cols * j:cols * j + cols].astype(BF)
                   for j in range(3))
        one_ref[one, 0:block, :] = q
        one_ref[one, block:block + cut, :] = k[:cut]
        two_ref[two, 0:rest, :] = k[cut:]
        two_ref[two, rest:rest + block, :] = v


clip_limit = 100.0
learn_rate = 0.08
vector_rate = 0.3
beta_one = 0.9
beta_two = 0.999
adam_eps = 1e-06
decay_rate = 0.01
step_count = 10


def adam_kernel(norm_ref, *refs):
    count = len(refs) // 7
    ins, outs = refs[:4 * count], refs[4 * count:]
    norm = norm_ref[0]
    factor = clip_limit / jnp.maximum(norm, clip_limit)
    fix_one = 1.0 - beta_one**step_count
    fix_two = 1.0 - beta_two**step_count
    for i in range(count):
        weight, first, second, grad = (r[...] for r in ins[4 * i:4 * i + 4])
        decay, rate = (decay_rate, learn_rate) if i < count - 1 else (0.0, vector_rate)
        c = factor * grad
        first_new = beta_one * first + (1.0 - beta_one) * c
        second_new = beta_two * second + (1.0 - beta_two) * c * c
        move = first_new / fix_one / (jnp.sqrt(second_new / fix_two) + adam_eps)
        outs[3 * i][...] = weight - rate * (move + decay * weight)
        outs[3 * i + 1][...] = first_new
        outs[3 * i + 2][...] = second_new


def adam(norm, groups):
    flat = [a for group in groups for a in group]
    shapes = [jax.ShapeDtypeStruct(group[0].shape, F32) for group in groups for _ in range(3)]
    full = lambda a: pl.BlockSpec(a.shape, lambda i: (0,) * len(a.shape))
    return pl.pallas_call(
        adam_kernel,
        grid=(1,),
        in_specs=[pl.BlockSpec(memory_space=pltpu.SMEM)] + [full(a) for a in flat],
        out_specs=[full(s) for s in shapes],
        out_shape=shapes,
        compiler_params=pltpu.CompilerParams(vmem_limit_bytes=32 << 20),
        name="adam",
    )(norm, *flat)


def grad_in_kernel(info, dz1_ref, own_ref, other_ref, w_ref, out_ref):
    out_ref[...] = dz1_ref[...] + nt(own_ref[...], w_ref[0]) + nt(other_ref[...], w_ref[1])


def grad_input(info, dz1, own, other, wqkv, tile=512):
    tok, model = dz1.shape
    width = own.shape[1]
    row = lambda d: pl.BlockSpec((tile, d), lambda s, info: (s, 0))
    return pl.pallas_call(
        grad_in_kernel,
        grid_spec=pltpu.PrefetchScalarGridSpec(
            num_scalar_prefetch=1,
            grid=(tok // tile,),
            in_specs=[row(model), row(width), row(width),
                      pl.BlockSpec(wqkv.shape, lambda s, info: (0, 0, 0))],
            out_specs=row(model),
        ),
        out_shape=jax.ShapeDtypeStruct((tok, model), F32),
        compiler_params=pltpu.CompilerParams(vmem_limit_bytes=40 << 20),
        name="grad_input",
    )(info, dz1, own, other, wqkv)


def core_swap(a):
    return lax.ppermute(a, "heads", [(0, 1), (1, 0)])


def by_core(core, own, other, axis):
    return jnp.where(core == 0, jnp.concatenate([own, other], axis), jnp.concatenate([other, own], axis))


def gather_plain(qkv_weight, out_weight, in_weight, back_weight):
    qkv = lax.all_gather(qkv_weight.astype(BF), "rows", axis=1, tiled=True)
    own = qkv.transpose(1, 0, 2).reshape(qkv.shape[1], -1)
    wqkv = jnp.stack([own, core_swap(own)])
    wo, w1, w2 = (
        lax.all_gather(w.astype(BF), ("rows", "heads"), axis=0, tiled=True)
        for w in (out_weight, in_weight, back_weight)
    )
    return wqkv, wo, w1, w2


def rows_swap(a, mask):
    return lax.ppermute(a, "rows", [(i, i ^ mask) for i in range(16)])


def gather_stream(shard, pieces_z, order):
    first, second = order
    base = jnp.concatenate([shard, *pieces_z], axis=0)
    one = rows_swap(base, first)
    two = rows_swap(base, second)
    three = rows_swap(one, second)
    own = (base, one, two, three)
    return own, tuple(core_swap(a) for a in own)


def gather_qkv(qkv_weight):
    shard = qkv_weight.astype(BF).reshape(-1, qkv_weight.shape[2])
    zs = [rows_swap(shard, z) for z in Z[1:]]
    cut = QKV_SPLIT[0]
    (own_a, other_a), (own_b, other_b) = (
        gather_stream(part(shard), [part(z) for z in zs], order)
        for part, order in zip((lambda a: a[:cut], lambda a: a[cut:]), STREAMS))
    return (*own_a, *own_b, *other_a, *other_b)


def gather_ffn(core, out_weight, in_weight, back_weight):
    def columns(which):
        pick = lambda a: lax.dynamic_slice_in_dim(a, which * (a.shape[1] // 2), a.shape[1] // 2, 1)
        return jnp.concatenate([pick(in_weight), pick(out_weight)], axis=1).astype(BF)

    chip = by_core(core, columns(core), core_swap(columns(1 - core)), 0)
    size = chip.shape[0]
    low = back_weight.astype(BF)
    shard = jnp.concatenate([chip, low[:size], low[size:]], axis=1)
    zs = [rows_swap(shard, z) for z in Z[1:]]
    cut = chip.shape[1]
    (own_a, other_a), (own_b, other_b) = (
        gather_stream(part(shard), [part(z) for z in zs], order)
        for part, order in zip((lambda a: a[:, :cut], lambda a: a[:, cut:]), STREAMS))
    return (*own_a, *own_b, *other_a, *other_b)


def total(*terms):
    return sum(a.astype(F32) for a in terms)


def reduce_stream(own, other, order):
    first, second = order
    kept = [own, core_swap(other)]
    low = lambda a, b: total(*(t[a:b] for t in kept)).astype(BF)
    kept.append(rows_swap(low(8, 16), first))
    kept.append(rows_swap(low(4, 8), second))
    last = [rows_swap(low(i, i + 1), Z[i]) for i in range(1, 4)]
    return total(*(t[0] for t in kept), *(t[0] for t in last))


def all_sum(a):
    a = a + core_swap(a)
    for mask in (1, 2, 4, 8):
        a = a + rows_swap(a, mask)
    return a


def body(n_rows, n_cores, tokens, cotangent, lengths, qkv_weight, qkv_first, qkv_second, out_weight, out_first,
         out_second, in_weight, in_first, in_second, back_weight, back_first, back_second,
         vectors, vector_first, vector_second):
    core = lax.axis_index("heads")
    row = lax.axis_index("rows")
    info = jnp.stack([core, row]).astype(jnp.int32)
    tok, model = cotangent.shape
    seq_len = tokens.shape[0] // lengths.shape[0]
    seqs = tok // seq_len
    cols = qkv_weight.shape[2]

    if n_rows == 16 and n_cores == 2 and model % 768 == 0:
        pieces = gather_qkv(qkv_weight)
        ffn_weights = gather_ffn(core, out_weight, in_weight, back_weight)
        ctx, q, k, v, lse, wqkv = attn_fwd(info, lengths, tokens, pieces, vectors, seqs, seq_len, cols)
        out, dz1, dctx, h, g, df, du, da, vec_grad, b1_grad = ffn(
            info, tokens, ctx, cotangent, ffn_weights, vectors)
        in_order, back_order = STREAMS
        back_grad_total = reduce_stream(*back_grad(info, g, df, back_order), back_order)
        wide_grad = reduce_stream(*in_grad(info, h, du, ctx, da, in_order), in_order)
        shapes = [jax.ShapeDtypeStruct((16, rows, cols), BF) for rows in QKV_SPLIT]
        (dq_other, bias_other, *other), (dq_own, bias_own, *own) = (
            attn_bwd(i, info, lengths, tokens, q, k, v, dctx, lse, seqs, seq_len, store_qkv, shapes)
            for i in (1, 0))
        qkv_grad = jnp.concatenate(
            [reduce_stream(a, b, order) for a, b, order in zip(own, other, STREAMS)], axis=0
        ).reshape(qkv_weight.shape)
        in_grad_total = wide_grad[:, :in_weight.shape[1]]
        out_grad = wide_grad[:, in_weight.shape[1]:]
        grads = (qkv_grad, out_grad, in_grad_total, back_grad_total)
        bias = by_core(core, bias_own[:2], bias_other[:2], 1)
        vector_part = jnp.concatenate([bias, vec_grad[:6], b1_grad.reshape(-1, model)], axis=0)
        square_part = sum(jnp.sum(a * a) for a in grads)
        sums = all_sum(jnp.concatenate([vector_part, jnp.full((1, model), square_part)], axis=0))
        vector_grad, square_total = sums[:-1], sums[-1, 0]
    else:
        wqkv, wo, w1, w2 = gather_plain(qkv_weight, out_weight, in_weight, back_weight)
        ctx, q, k, v, lse = attn_fwd(
            info, lengths, tokens, (wqkv,), vectors, seqs, seq_len, cols)
        out, dz1, dctx, h, g, df, du, da, vec_grad, b1_grad = ffn(
            info, tokens, ctx, cotangent, (wo, w1, w2), vectors)
        dw2 = tn(g, df)
        dw1 = tn(h, du)
        dwo = tn(ctx, da)
        both = [attn_bwd(i, info, lengths, tokens, q, k, v, dctx, lse, seqs, seq_len) for i in (1, 0)]
        (dq_other, bias_other), (dq_own, bias_own) = both
        x_half = lax.dynamic_slice_in_dim(tokens, core * tok, tok, 0)
        dqkv = tn(x_half, dq_own) + core_swap(tn(x_half, dq_other))
        qkv_grad = lax.psum_scatter(dqkv, "rows", scatter_dimension=0, tiled=True)
        qkv_grad = qkv_grad.reshape(-1, 3, cols).transpose(1, 0, 2)
        grads = tuple(
            lax.psum_scatter(a, ("rows", "heads"), scatter_dimension=0, tiled=True)
            for a in (dwo, dw1, dw2)
        )
        bias = by_core(core, bias_own[:2], bias_other[:2], 1)
        vector_part = jnp.concatenate([bias, vec_grad[:6], b1_grad.reshape(-1, model)], axis=0)
        grads = (qkv_grad, *grads)
        square_part = sum(jnp.sum(a * a) for a in grads)
        vector_grad, square_total = lax.psum((vector_part, square_part), ("rows", "heads"))
    norm = jnp.sqrt(square_total + jnp.sum(vector_grad * vector_grad)).reshape(1)
    grad_in = grad_input(info, dz1, dq_own, dq_other, wqkv)
    new = adam(norm, [
        (qkv_weight, qkv_first, qkv_second, grads[0]),
        (out_weight, out_first, out_second, grads[1]),
        (in_weight, in_first, in_second, grads[2]),
        (back_weight, back_first, back_second, grads[3]),
        (vectors, vector_first, vector_second, vector_grad),
    ])
    return (out, grad_in, norm, *new)


def solution(mesh):
    split = P(("rows", "heads"), None)
    qkv = P(None, "rows", "heads")
    weights = (qkv,) * 3 + (split,) * 9 + (P(),) * 3
    return jax.shard_map(
        lambda *args: body(mesh.shape["rows"], mesh.shape["heads"], *args),
        mesh=mesh,
        in_specs=(P("rows", None), split, P("rows")) + weights,
        out_specs=(split, split, P()) + weights,
        check_vma=False,
    )
```
